256 devices in a mesh: dp: 4 (over y), ctx: 64 (over z, x, core).
Axes of the slice: x: 4, y: 4, z: 8, core: 2. Of those that a mesh axis runs over, the one named last changes fastest.
Arguments:
- queries: bfloat16 [32768, 2048], P(('dp', 'ctx')), parts along dimension 0, may hold values from -6 to 6
- keys: bfloat16 [32768, 2048], P(('dp', 'ctx')), parts along dimension 0, may hold values from -6 to 6
- values_in: bfloat16 [32768, 2048], P(('dp', 'ctx')), parts along dimension 0, may hold values from -6 to 6
- conv_weights: float32 [4, 6144], replicated, may hold values from -3 to 3
- log_gates: float32 [16, 32768], P(None, ('dp', 'ctx')), parts along dimension 1, may hold values from -0.7 to 0
- betas: float32 [16, 32768], P(None, ('dp', 'ctx')), parts along dimension 1, may hold values from 0 to 0.9
- level_weights: float32 [7, 16, 32768], P(None, None, ('dp', 'ctx')), parts along dimension 2, may hold values from 0.1 to 4
- doc_lengths: int32 [24], P('dp'), parts along dimension 0, may hold values from 1 to 4096, 8192 in all
- out_gain: float32 [2048], replicated, may hold values from 0.1 to 1.9
Outputs:
- mixed: bfloat16 [32768, 2048], P(('dp', 'ctx')), parts along dimension 0
The draws below stay inside these ranges and needn't reach their ends.
There are 4 independent parts, one for each index of `dp`. The reference program is written for one: setup_inputs(seed, part) draws one part's arguments, and reference() takes and returns one part's arrays. A program takes and returns all parts, laid end to end along the dimension named above; an argument that names none is the same for every part. Nothing has to cross between parts.
Inputs may be any that keep to these rules, and one draw needn't show every extreme that they name: `doc_lengths`: the documents tile the 8192 tokens of a sequence; the longest has exactly 4096 tokens.
All inputs are finite; a program needn't handle non-finite values.
Results may differ from the reference program's by a relative error of at most 0.0011.
Values may be sent and summed in bfloat16 or wider, within the bound.
A program may use at most 64 MiB of HBM per device.

```python
import math
import jax
import jax.numpy as jnp
import numpy as np
from jax import lax

HEAD_TOTAL = 16
DK = 128
DV = 128
KCONV = 4
LEVELS = 7
DOCS = 6
TOK_DEV = 128
SEQUENCE_TOKENS = 8192
N_CTX = 64


def head_roles(key):
    fast_count = HEAD_TOTAL - HEAD_TOTAL // 2
    slow_count = HEAD_TOTAL - fast_count
    head_rank = jax.random.permutation(jax.random.fold_in(key, 11), HEAD_TOTAL)
    slow_head = head_rank < slow_count
    fast_place = jnp.maximum(head_rank - slow_count, 0).astype(jnp.float32)
    return (slow_head, fast_place, fast_count)


def draw_log_gates(key, part):
    slow_head, fast_place, fast_count = head_roles(key)
    every_key = jax.random.split(jax.random.fold_in(key, 21), 5)
    jitter = jnp.exp(jax.random.uniform(every_key[0], (HEAD_TOTAL, SEQUENCE_TOKENS), minval=-0.693, maxval=0.693))
    slab_factor = jnp.exp(jax.random.uniform(every_key[1], (HEAD_TOTAL, SEQUENCE_TOKENS // TOK_DEV, 1), minval=-0.693, maxval=0.693))
    slab_factor = jnp.broadcast_to(slab_factor, (HEAD_TOTAL, SEQUENCE_TOKENS // TOK_DEV, TOK_DEV)).reshape(HEAD_TOTAL, SEQUENCE_TOKENS)
    short_time = 40.0
    long_time = 160.0
    offset_draw = jax.random.uniform(every_key[2], (HEAD_TOTAL,))
    position = (fast_place + offset_draw) / fast_count
    log_time = math.log(short_time) + (math.log(long_time) - math.log(short_time)) * position
    fast_rate = jnp.exp(-log_time)[:, None]
    slow_rate = 0.4 / SEQUENCE_TOKENS
    decay_speed = jnp.where(slow_head[:, None], slow_rate, fast_rate) * jitter * slab_factor
    marked_positions = jax.random.randint(every_key[3], (HEAD_TOTAL, 3), 0, SEQUENCE_TOKENS)
    sudden_pulse = jnp.any(jnp.arange(SEQUENCE_TOKENS)[None, None, :] == marked_positions[:, :, None], axis=1)
    pulse_value = jnp.log(jax.random.uniform(every_key[4], (HEAD_TOTAL, SEQUENCE_TOKENS), minval=0.5, maxval=0.8))
    return jnp.where(sudden_pulse, pulse_value, -decay_speed).astype(jnp.float32)


def draw_betas(key, part):
    slow_head, fast_place, fast_count = head_roles(key)
    every_key = jax.random.split(jax.random.fold_in(key, 31), 2)
    slow_value = jax.random.uniform(every_key[0], (HEAD_TOTAL, SEQUENCE_TOKENS), minval=0.03, maxval=0.049)
    fast_value = jax.random.uniform(every_key[1], (HEAD_TOTAL, SEQUENCE_TOKENS), minval=0.2, maxval=0.9)
    return jnp.where(slow_head[:, None], slow_value, fast_value).astype(jnp.float32)


def draw_level_weights(key, part):
    every_key = jax.random.split(jax.random.fold_in(key, 41), 2)
    shape_all = (LEVELS, HEAD_TOTAL, SEQUENCE_TOKENS)
    near_part = jnp.exp(jax.random.uniform(every_key[0], shape_all, minval=math.log(0.1), maxval=math.log(0.2)))
    far_part = jnp.exp(jax.random.uniform(every_key[1], shape_all, minval=math.log(2.0), maxval=math.log(4.0)))
    level_index = jnp.arange(LEVELS)[:, None, None]
    chosen = jnp.where(level_index < LEVELS - 3, near_part, far_part)
    return jnp.clip(chosen, 0.1, 4.0).astype(jnp.float32)


def shard_levels(stream_key, dims, cuts, low, high):
    def one(dim, parts):
        heights = jax.random.uniform(jax.random.fold_in(jax.random.fold_in(stream_key, 6), dim), (parts,), jnp.float32, low / len(cuts), high / len(cuts))
        return jnp.repeat(jnp.exp(heights), dims[dim] // parts).reshape((-1,) + (1,) * (len(dims) - dim - 1))

    factor_of = one(*cuts[0])
    for cut in cuts[1:]:
        factor_of = factor_of * one(*cut)
    return factor_of


def profile(count, total, most, slope):
    weights = [(1 << 20) // math.isqrt(grade ** slope) + 1 for grade in range(2, count + 1)]
    surplus, holding = total - most - (count - 1), [1] * (count - 1)
    while surplus > 0:
        candidates = [i for i in range(count - 1) if holding[i] < most]
        pool, left = sum([weights[i] for i in candidates]), surplus
        for i in candidates:
            addition = min(most - holding[i], max(1, left * weights[i] // pool), surplus)
            holding[i] = holding[i] + addition
            surplus = surplus - addition
    return np.array([most] + holding)


def ragged(stream_key, number_of, total, most, lean):
    if number_of == 2:
        one = jax.random.randint(stream_key, (), max(1, total - most), min(most, total - 1) + 1)
        return jnp.stack([one, total - one])
    lengths = jnp.asarray(profile(number_of, total, most, lean), jnp.int32)
    twos = (number_of - 1) // 2
    donor, sink = lengths[1:1 + 2 * twos:2], lengths[2:2 + 2 * twos:2]
    margin = jnp.minimum(donor - 1, most - sink)
    passed = jax.random.randint(jax.random.fold_in(stream_key, 1), (twos,), 0, 1 << 20) % (margin + 1)
    lengths = lengths.at[1:1 + 2 * twos:2].set(donor - passed).at[2:2 + 2 * twos:2].set(sink + passed)
    return lengths[jax.random.permutation(jax.random.fold_in(stream_key, 2), number_of)]


def normal_values(key, shape, scale, reach, shards=(), kind=jnp.bfloat16):
    loudness = shard_levels(key, shape, shards, -0.22, 0.18) if shards else 1.0
    result = jax.random.normal(key, shape, jnp.float32) * scale * loudness
    return jnp.minimum(jnp.maximum(result, -reach), reach).astype(kind)


def setup_inputs(seed: int = 0, part: int = 0) -> dict:
    streams_of = jax.random.split(jax.random.key(seed), 10)
    own_keys = jax.random.split(jax.random.fold_in(streams_of[9], part), 10)
    queries = normal_values(own_keys[0], (SEQUENCE_TOKENS, HEAD_TOTAL * DK), 1.0, 6.0, ((0, 64),))
    keys = normal_values(own_keys[1], (SEQUENCE_TOKENS, HEAD_TOTAL * DK), 1.0, 6.0, ((0, 64),))
    values_in = normal_values(own_keys[2], (SEQUENCE_TOKENS, HEAD_TOTAL * DV), 1.0, 6.0, ((0, 64),))
    conv_weights = normal_values(streams_of[3], (KCONV, 2 * HEAD_TOTAL * DK + HEAD_TOTAL * DV), 0.5, 3.0, (), jnp.float32)
    log_gates = draw_log_gates(jax.random.fold_in(jax.random.fold_in(streams_of[9], part), 71), part)
    betas = draw_betas(jax.random.fold_in(jax.random.fold_in(streams_of[9], part), 71), part)
    level_weights = draw_level_weights(jax.random.fold_in(jax.random.fold_in(streams_of[9], part), 71), part)
    doc_lengths = ragged(own_keys[7], DOCS, SEQUENCE_TOKENS, SEQUENCE_TOKENS // 2, 2).astype(jnp.int32)
    out_gain = jnp.clip(1.0 + 0.18 * jax.random.normal(streams_of[8], (HEAD_TOTAL * DV,), jnp.float32), 0.1, 1.9)
    return {"queries": queries, "keys": keys, "values_in": values_in, "conv_weights": conv_weights, "log_gates": log_gates, "betas": betas, "level_weights": level_weights, "doc_lengths": doc_lengths, "out_gain": out_gain}


def tap_mask(starts, first_pos, count, taps):
    extent = first_pos - (taps - 1) + jnp.arange(count + taps - 1, dtype=jnp.int32)
    doc_ext = lax.optimization_barrier(jnp.sum((starts[None, :] <= extent[:, None]).astype(jnp.int32), axis=1)) - 1
    target = doc_ext[taps - 1:]
    columns = [(doc_ext[taps - 1 - offset:taps - 1 - offset + count] == target).astype(jnp.float32) for offset in range(taps)]
    return jnp.stack(columns, axis=1)

def reset_flags(starts, first_pos, count):
    position = first_pos + jnp.arange(count, dtype=jnp.int32)
    return jnp.any(position[:, None] == starts[None, :], axis=1).astype(jnp.float32)

def conv_silu(extended, weights, valid):
    taps = weights.shape[0]
    count = valid.shape[0]
    total = jnp.zeros((count, extended.shape[1]), jnp.float32)
    for offset in range(taps):
        rows = extended[taps - 1 - offset:taps - 1 - offset + count].astype(jnp.float32)
        total = total + weights[offset][None, :] * rows * valid[:, offset:offset + 1]
    return jax.nn.silu(total)

def split_heads(flat, heads):
    return flat.reshape(flat.shape[0], heads, -1).transpose(1, 0, 2)

def unit_rows(matrix):
    return matrix * lax.rsqrt(lax.optimization_barrier(jnp.sum(matrix * matrix, axis=-1, keepdims=True)) + 1e-06)

def solve_lower(system, rhs):
    return jax.scipy.linalg.solve_triangular(system, rhs, lower=True, unit_diagonal=True)

def slab_terms(qnorm, knorm, values, gates, strengths, resets):
    count = qnorm.shape[1]
    width = knorm.shape[2]
    highest = lax.Precision.HIGHEST
    segment = jnp.cumsum(resets)
    rows = jnp.arange(count, dtype=jnp.int32)
    keep = (segment[:, None] == segment[None, :]) & (rows[:, None] >= rows[None, :])
    strict = (rows[:, None] > rows[None, :]).astype(jnp.float32)
    cumulative = jnp.cumsum(gates, axis=1)
    spread = cumulative[:, :, None] - cumulative[:, None, :]
    decay = jnp.where(keep[None], jnp.exp(jnp.where(keep[None], spread, 0.0)), 0.0)
    alive = (segment == 0.0).astype(jnp.float32)
    head_decay = jnp.exp(cumulative) * alive[None, :]
    key_key = jnp.einsum('hti,hsi->hts', knorm, knorm, precision=highest)
    system = jnp.eye(count, dtype=jnp.float32)[None] + decay * key_key * strengths[:, :, None] * strict[None]
    rhs_keys = (strengths * head_decay)[:, :, None] * knorm
    rhs_values = strengths[:, :, None] * values
    solved = jax.vmap(solve_lower)(system, jnp.concatenate([rhs_keys, rhs_values], axis=2))
    key_part = solved[:, :, :width]
    value_part = solved[:, :, width:]
    query_key = decay * jnp.einsum('hti,hsi->hts', qnorm, knorm, precision=highest)
    local = jnp.einsum('hts,hsv->htv', query_key, value_part, precision=highest)
    qeff = head_decay[:, :, None] * qnorm - jnp.einsum('hts,hsi->hti', query_key, key_part, precision=highest)
    last_row = decay[:, count - 1, :]
    weighted = knorm * last_row[:, :, None]
    trans = head_decay[:, count - 1][:, None, None] * jnp.eye(width, dtype=jnp.float32)[None] - jnp.einsum('hsi,hsj->hij', weighted, key_part, precision=highest)
    written = jnp.einsum('hsi,hsv->hiv', weighted, value_part, precision=highest)
    return (local, qeff, trans, written)

def finish(heads_out, gain):
    scaled = heads_out * lax.rsqrt(lax.optimization_barrier(jnp.mean(heads_out * heads_out, axis=-1, keepdims=True)) + 1e-06)
    merged = scaled.transpose(1, 0, 2).reshape(heads_out.shape[1], -1)
    return (merged * gain[None, :]).astype(jnp.bfloat16)

def bit_length(number):
    total = jnp.zeros((), jnp.int32)
    for place in range(24):
        total = total + (jnp.right_shift(number, place) > 0).astype(jnp.int32)
    return total

def reference(queries, keys, values_in, conv_weights, log_gates, betas, level_weights, doc_lengths, out_gain):
    taps = KCONV
    width_k = HEAD_TOTAL * DK
    starts = (jnp.cumsum(doc_lengths) - doc_lengths).astype(jnp.int32)
    padded_q = jnp.pad(queries, ((taps - 1, 0), (0, 0)))
    padded_k = jnp.pad(keys, ((taps - 1, 0), (0, 0)))
    padded_v = jnp.pad(values_in, ((taps - 1, 0), (0, 0)))
    highest = lax.Precision.HIGHEST

    def step(levels, index):
        first = (index * TOK_DEV).astype(jnp.int32)
        valid = tap_mask(starts, first, TOK_DEV, taps)
        resets = reset_flags(starts, first, TOK_DEV)
        conv_q = conv_silu(lax.dynamic_slice_in_dim(padded_q, first, TOK_DEV + taps - 1, 0), conv_weights[:, :width_k], valid)
        conv_k = conv_silu(lax.dynamic_slice_in_dim(padded_k, first, TOK_DEV + taps - 1, 0), conv_weights[:, width_k:2 * width_k], valid)
        conv_v = conv_silu(lax.dynamic_slice_in_dim(padded_v, first, TOK_DEV + taps - 1, 0), conv_weights[:, 2 * width_k:], valid)
        qnorm = unit_rows(split_heads(conv_q, HEAD_TOTAL)) * DK ** (-0.5)
        knorm = unit_rows(split_heads(conv_k, HEAD_TOTAL))
        values = split_heads(conv_v, HEAD_TOTAL)
        gates = lax.dynamic_slice_in_dim(log_gates, first, TOK_DEV, 1)
        strengths = lax.dynamic_slice_in_dim(betas, first, TOK_DEV, 1)
        weights_here = lax.dynamic_slice_in_dim(level_weights, first, TOK_DEV, 2)
        local, qeff, trans, written = slab_terms(qnorm, knorm, values, gates, strengths, resets)
        heads_out = weights_here[0][:, :, None] * local
        for level in range(1, LEVELS):
            heads_out = heads_out + weights_here[level][:, :, None] * jnp.einsum('hti,hiv->htv', qeff, levels[level], precision=highest)
        block = finish(heads_out, out_gain)
        moved = jnp.einsum('hij,lhjv->lhiv', trans, levels, precision=highest)
        target = jnp.minimum(bit_length(jnp.bitwise_xor(index, index + 1)), LEVELS - 1)
        ranks = jnp.arange(LEVELS, dtype=jnp.int32)[:, None, None, None]
        merged = lax.optimization_barrier(jnp.sum(jnp.where(ranks <= target, moved, 0.0), axis=0)) + written
        fresh = jnp.where(ranks == target, merged[None], jnp.where(ranks < target, 0.0, moved))
        return (fresh, block)
    initial = jnp.zeros((LEVELS, HEAD_TOTAL, DK, DV), jnp.float32)
    final_levels, blocks = lax.scan(step, initial, jnp.arange(N_CTX, dtype=jnp.int32))
    return blocks.reshape(SEQUENCE_TOKENS, HEAD_TOTAL * DV)
```

```python
import functools
import jax
import jax.numpy as jnp
from jax import lax
from jax.experimental import pallas as pl
from jax.experimental.pallas import tpu as pltpu
from jax.sharding import PartitionSpec as P

F32 = jnp.float32
BF16 = jnp.bfloat16
C = 128
SEG = 16
NB = 4


def halves(x):
    high = x.astype(BF16)
    low = (x - high.astype(F32)).astype(BF16)
    return high, low


def left_form(x):
    return jnp.concatenate(halves(x), axis=1)


def right_form(x):
    high, low = halves(x)
    wide = jnp.concatenate([high, low], axis=1)
    return jnp.concatenate([wide, wide], axis=0)


def times(left, right):
    r = jnp.dot(left, right, preferred_element_type=F32)
    return r[:, :C] + r[:, C:]


def lanes_ds(i):
    return pl.ds(pl.multiple_of(i * C, C), C)


def fill_rows(first, doc_ref, scal_ref, rows_ref):
    bounds = []
    acc = jnp.int32(0)
    for i in range(doc_ref.shape[0]):
        bounds.append(acc)
        acc = acc + doc_ref[i]
    pos = first + lax.broadcasted_iota(jnp.int32, (SEG, C), 0) * C + lax.broadcasted_iota(jnp.int32, (SEG, C), 1)
    slab_pos = first + lax.broadcasted_iota(jnp.int32, (SEG, C), 0) * C - 1

    def doc_of(p):
        total = jnp.zeros((SEG, C), F32)
        for b in bounds:
            total = total + jnp.where(p >= b, 1.0, 0.0)
        return total

    doc = doc_of(pos)
    upper = (lax.broadcasted_iota(jnp.int32, (C, C), 0) <= lax.broadcasted_iota(jnp.int32, (C, C), 1)).astype(F32)
    cum = jnp.dot(scal_ref[:, 0, :], upper, precision=lax.Precision.HIGHEST, preferred_element_type=F32)
    rows_ref[:, 0, :] = cum
    rows_ref[:, 1, :] = scal_ref[:, 1, :]
    for l in range(7):
        rows_ref[:, 2 + l, :] = scal_ref[:, 2 + l, :]
    rows_ref[:, 9, :] = doc
    rows_ref[:, 10, :] = jnp.where(doc == doc_of(slab_pos), jnp.exp(cum), 0.0)
    for m in (1, 2, 3):
        rows_ref[:, 10 + m, :] = jnp.where(doc == doc_of(pos - m), 1.0, 0.0)
    rows_ref[:, 14, :] = jnp.zeros((SEG, C), F32)
    rows_ref[:, 15, :] = jnp.zeros((SEG, C), F32)


def conv(ext, taps, valid):
    x = ext.astype(F32)
    total = taps[0:1] * x[16:]
    for m in (1, 2, 3):
        total = total + taps[m : m + 1] * x[16 - m : 144 - m] * valid[m - 1]
    return total / (1.0 + jnp.exp(-total))


def slab_group(js, taps, rows_ref, x_ref, rim_ref, local_ref, qeff_ref, trans_ref, write_ref):
    it = lax.broadcasted_iota(jnp.int32, (C, C), 0)
    js_ = lax.broadcasted_iota(jnp.int32, (C, C), 1)
    lower = it >= js_
    apart = jnp.where(it > js_, it ^ js_, 0)
    eye = jnp.where(it == js_, 1.0, 0.0)
    n = len(js)
    q, k, v, cols, rows = [], [], [], [], []
    for j in js:
        r = rows_ref[j]
        c = r.T
        rows.append(r)
        cols.append(c)
        valid = [c[:, 10 + m : 11 + m] for m in (1, 2, 3)]
        cq, ck, cv = [conv(jnp.concatenate([rim_ref[j, a], x_ref[j, a]], axis=0), taps[a], valid) for a in range(3)]
        q.append(cq * (lax.rsqrt(jnp.sum(cq * cq, axis=1, keepdims=True) + 1e-06) * C ** (-0.5)))
        k.append(ck * lax.rsqrt(jnp.sum(ck * ck, axis=1, keepdims=True) + 1e-06))
        v.append(cv)
    kt = [x.T for x in k]
    gram = [times(left_form(jnp.concatenate([q[i], k[i]], axis=0)), right_form(kt[i])) for i in range(n)]
    outer, system = [], []
    for i in range(n):
        r, c = rows[i], cols[i]
        keep = lower & (c[:, 9:10] == r[9:10])
        decay = jnp.exp(jnp.where(keep, c[:, 0:1] - r[0:1], -1e30))
        beta = r[1:2]
        outer.append(jnp.concatenate([decay * gram[i][:C], kt[i] * decay[C - 1 : C]], axis=0) * beta)
        system.append(decay * gram[i][C:] * beta)
    inverse = [eye - jnp.where(apart == 1, system[i], 0.0) for i in range(n)]
    b = 2
    while b < C:
        pick = (apart >= b) & (apart < 2 * b)
        half = [times(left_form(inverse[i]), right_form(jnp.where(pick, system[i], 0.0))) for i in range(n)]
        inverse = [inverse[i] - times(left_form(half[i]), right_form(inverse[i])) for i in range(n)]
        b *= 2
    mixed = [left_form(times(left_form(outer[i]), right_form(inverse[i]))) for i in range(n)]
    for i in range(n):
        hd = cols[i][:, 10:11]
        with_v = times(mixed[i], right_form(v[i]))
        with_k = times(mixed[i], right_form(k[i] * hd))
        local_ref[js[i]] = with_v[:C] * cols[i][:, 2:3]
        write_ref[js[i]] = with_v[C:]
        qeff_ref[js[i]] = q[i] * hd - with_k[:C]
        trans_ref[js[i]] = rows[i][10:11, C - 1 : C] * eye - with_k[C:]


def scan_half(part, levels, prefix, rows_ref, local_ref, qeff_ref, trans_ref, write_ref, reach_ref):
    for j in range(part * SEG // 2, (part + 1) * SEG // 2):
        trans = trans_ref[j]
        qeff = qeff_ref[j]
        moved = {}
        if j:
            both = left_form(jnp.concatenate([qeff, trans], axis=0))
            c = rows_ref[j].T
            total = local_ref[j]
            for l, state in levels.items():
                r = times(both, right_form(state))
                total = total + r[:C] * c[:, 2 + l : 3 + l]
                moved[l] = r[C:]
            local_ref[j] = total
            r = times(both, right_form(prefix))
            reach_ref[j] = r[:C]
            prefix = r[C:]
        else:
            reach_ref[j] = qeff
            prefix = trans
        target = (j ^ (j + 1)).bit_length()
        merged = write_ref[j]
        for l in list(moved):
            if l <= target:
                merged = merged + moved.pop(l)
        moved[target] = merged
        levels = moved
    return levels, prefix


def block_totals(trans_ref, write_ref, seg_ref):
    blocks = [(trans_ref[j], write_ref[j]) for j in range(SEG)]
    while len(blocks) > 1:
        joined = []
        for a in range(0, len(blocks), 2):
            upper = left_form(blocks[a + 1][0])
            joined.append((
                times(upper, right_form(blocks[a][0])),
                times(upper, right_form(blocks[a][1])) + blocks[a + 1][1],
            ))
        blocks = joined
    seg_ref[0] = blocks[0][0]
    seg_ref[1] = blocks[0][1]


def final(j, s5, s6, gain, rows_ref, local_ref, reach_ref):
    c = rows_ref[j].T
    reach = left_form(reach_ref[j])
    o = local_ref[j] + times(reach, s5) * c[:, 7:8] + times(reach, s6) * c[:, 8:9]
    return (o * lax.rsqrt(jnp.mean(o * o, axis=1, keepdims=True) + 1e-06) * gain).astype(BF16)


def kernel(
    doc_ref, cw_ref, gain_ref, scal_src, q_src, k_src, v_src, out_ref,
    x_ref, rim_ref, scal_ref, rows_ref, local_ref, qeff_ref, trans_ref, write_ref, reach_ref,
    seg_ref, far_ref, joint_ref, states_ref, stage_ref,
    in_send, in_recv, rim_send, rim_recv, far_send, far_recv, out_send, out_recv,
):
    me = lax.axis_index("ctx")
    segment = lax.div(me, SEG)
    mine = lax.rem(me, SEG)
    my_z, my_x, my_core = lax.div(mine, 8), lax.rem(lax.div(mine, 2), 4), lax.rem(mine, 2)

    def place(dz, dx, dc):
        return lax.rem(my_z + dz, 2) * 8 + lax.rem(my_x + dx, 4) * 2 + lax.rem(my_core + dc, 2)

    def at(seg, head):
        return {"ctx": lax.rem(seg, 4) * SEG + head}

    barrier = pltpu.get_barrier_semaphore()

    def greet(target):
        pl.semaphore_signal(barrier, inc=1, device_id=target, device_id_type=pl.DeviceIdType.MESH)

    for n in range(1, SEG):
        greet(at(segment, lax.rem(mine + n, SEG)))
    for n in range(1, 4):
        greet(at(segment + n, mine))
    greet(at(segment + 3, SEG - 1))

    @pl.when(mine == SEG - 1)
    def _():
        for n in range(SEG):
            greet(at(segment + 1, n))
        pl.semaphore_wait(barrier, 19 + SEG)

    @pl.when(mine != SEG - 1)
    def _():
        pl.semaphore_wait(barrier, 19)

    sources = (q_src, k_src, v_src)

    def piece(a, src, dst, head, slab):
        if a == 3:
            return scal_src.at[head], scal_ref.at[slab]
        return sources[a].at[:, lanes_ds(head)], x_ref.at[slab, a]

    def sending(a, head):
        src, dst = piece(a, None, None, head, mine)
        return pltpu.make_async_remote_copy(
            src_ref=src, dst_ref=dst, send_sem=in_send.at[head, a], recv_sem=in_recv.at[mine, a],
            device_id=at(segment, head), device_id_type=pl.DeviceIdType.MESH,
        )

    def keeping(a):
        src, dst = piece(a, None, None, mine, mine)
        return pltpu.make_async_copy(src, dst, in_recv.at[mine, a])

    def arriving(a, slab):
        src, dst = piece(a, None, None, mine, slab)
        return pltpu.make_async_remote_copy(
            src_ref=src, dst_ref=dst, send_sem=in_send.at[slab, a], recv_sem=in_recv.at[slab, a],
            device_id=at(segment, slab), device_id_type=pl.DeviceIdType.MESH,
        )

    follower = lax.rem(mine + 1, SEG)

    def rim(a, head, slot, seg):
        return pltpu.make_async_remote_copy(
            src_ref=sources[a].at[pl.ds(C - 16, 16), lanes_ds(head)], dst_ref=rim_ref.at[slot, a],
            send_sem=rim_send.at[head, a], recv_sem=rim_recv.at[slot, a],
            device_id=at(seg, head), device_id_type=pl.DeviceIdType.MESH,
        )

    def own_rim(a):
        return pltpu.make_async_copy(
            sources[a].at[pl.ds(C - 16, 16), lanes_ds(mine)], rim_ref.at[follower, a], rim_recv.at[follower, a]
        )

    def rims_out(act):
        @pl.when(mine == SEG - 1)
        def _():
            for n in range(SEG):
                for a in range(3):
                    act(rim(a, jnp.int32(n), follower, segment + 1))

        @pl.when(mine != SEG - 1)
        def _():
            for step in order:
                for a in range(3):
                    act(rim(a, place(*step), follower, segment))

    def await_rim(slot):
        local = slot == mine + 1

        @pl.when(local)
        def _():
            for a in range(3):
                own_rim(a).wait()

        @pl.when(jnp.logical_not(local))
        def _():
            for a in range(3):
                rim(a, mine, slot, segment).wait_recv()

    for a in range(4):
        keeping(a).start()
    order = [(dz, dx, dc) for dx in (0, 1, 3, 2) for dz in (0, 1) for dc in (0, 1)][1:]
    for step in order:
        sending(3, place(*step)).start()
    rims_out(lambda copy: copy.start())

    @pl.when(mine != SEG - 1)
    def _():
        for a in range(3):
            own_rim(a).start()

    for step in order:
        for a in range(3):
            sending(a, place(*step)).start()

    keeping(3).wait()
    for step in order:
        arriving(3, place(step[0], (4 - step[1]) % 4, step[2])).wait_recv()
    fill_rows(segment * (SEG * C), doc_ref, scal_ref, rows_ref)
    for a in range(3):
        keeping(a).wait()

    taps = [cw_ref[:, lanes_ds(SEG * a + mine)] for a in range(3)]

    def group(m, _):
        dx = m + lax.div(m, 2) - 2 * lax.div(m, 3)
        js = [place(dz, 4 - dx, dc) for dz in (0, 1) for dc in (0, 1)]
        for n, j in enumerate(js):
            if n:
                for a in range(3):
                    arriving(a, j).wait_recv()
            else:
                @pl.when(m > 0)
                def _():
                    for a in range(3):
                        arriving(a, j).wait_recv()
        for j in js:
            await_rim(j)
        slab_group(js, taps, rows_ref, x_ref, rim_ref, local_ref, qeff_ref, trans_ref, write_ref)
        return 0

    lax.fori_loop(0, SEG // NB, group, 0)

    def across(n, src, to):
        return pltpu.make_async_remote_copy(
            src_ref=src, dst_ref=far_ref.at[n], send_sem=far_send.at[n], recv_sem=far_recv.at[n],
            device_id=at(jnp.int32(to), mine), device_id_type=pl.DeviceIdType.MESH,
        )

    block_totals(trans_ref, write_ref, seg_ref)
    first_write = across(0, seg_ref.at[1], 1)
    third_trans = across(1, seg_ref.at[0], 3)
    third_write = across(2, seg_ref.at[1], 3)
    to_third = across(3, joint_ref, 2)
    to_fourth = pltpu.make_async_remote_copy(
        src_ref=joint_ref, dst_ref=far_ref.at[3], send_sem=far_send.at[4], recv_sem=far_recv.at[3],
        device_id=at(jnp.int32(3), mine), device_id_type=pl.DeviceIdType.MESH,
    )

    @pl.when(segment == 0)
    def _():
        first_write.start()

    @pl.when(segment == 2)
    def _():
        third_trans.start()
        third_write.start()

    levels, prefix = scan_half(0, {}, None, rows_ref, local_ref, qeff_ref, trans_ref, write_ref, reach_ref)

    states_ref[...] = jnp.zeros_like(states_ref)

    @pl.when(segment == 1)
    def _():
        first_write.wait_recv()
        states_ref[0] = far_ref[0]
        joint_ref[...] = times(left_form(seg_ref[0]), right_form(far_ref[0])) + seg_ref[1]
        to_third.start()
        to_fourth.start()

    scan_half(1, levels, prefix, rows_ref, local_ref, qeff_ref, trans_ref, write_ref, reach_ref)

    @pl.when(segment == 2)
    def _():
        to_third.wait_recv()
        states_ref[1] = far_ref[3]

    @pl.when(segment == 3)
    def _():
        third_trans.wait_recv()
        third_write.wait_recv()
        states_ref[0] = far_ref[2]
        to_fourth.wait_recv()
        states_ref[1] = times(left_form(far_ref[1]), right_form(far_ref[3]))

    gain = gain_ref[:, lanes_ds(mine)]
    s5 = right_form(states_ref[0])
    s6 = right_form(states_ref[1])

    def leaving(slab):
        return pltpu.make_async_remote_copy(
            src_ref=stage_ref.at[slab], dst_ref=out_ref.at[:, lanes_ds(mine)],
            send_sem=out_send.at[slab], recv_sem=out_recv.at[mine],
            device_id=at(segment, slab), device_id_type=pl.DeviceIdType.MESH,
        )

    def returning(head):
        return pltpu.make_async_remote_copy(
            src_ref=stage_ref.at[head], dst_ref=out_ref.at[:, lanes_ds(head)],
            send_sem=out_send.at[head], recv_sem=out_recv.at[head],
            device_id=at(segment, head), device_id_type=pl.DeviceIdType.MESH,
        )

    for dx in (2, 1, 3, 0):
        js = [place(dz, dx, dc) for dz in (1, 0) for dc in (1, 0)]
        for j in js:
            stage_ref[j] = final(j, s5, s6, gain, rows_ref, local_ref, reach_ref)
        for j in js[: 4 if dx else 3]:
            leaving(j).start()
    home = pltpu.make_async_copy(stage_ref.at[mine], out_ref.at[:, lanes_ds(mine)], out_recv.at[mine])
    home.start()
    home.wait()
    for step in order:
        returning(place(*step)).wait_recv()

    for step in order:
        head = place(*step)
        for a in range(4):
            sending(a, head).wait_send()
        leaving(head).wait_send()

    rims_out(lambda copy: copy.wait_send())

    @pl.when(segment == 0)
    def _():
        first_write.wait_send()

    @pl.when(segment == 1)
    def _():
        to_third.wait_send()
        to_fourth.wait_send()

    @pl.when(segment == 2)
    def _():
        third_trans.wait_send()
        third_write.wait_send()


def body(queries, keys, values_in, conv_weights, log_gates, betas, level_weights, doc_lengths, out_gain):
    heads, count = log_gates.shape
    scal = jnp.concatenate(
        [log_gates[None], betas[None], level_weights, jnp.zeros((7, heads, count), F32)], axis=0
    ).transpose(1, 0, 2)
    square = pltpu.VMEM((SEG, C, C), F32)
    hbm = pl.BlockSpec(memory_space=pl.ANY)
    vmem = pl.BlockSpec(memory_space=pltpu.VMEM)
    dma = pltpu.SemaphoreType.DMA
    return pl.pallas_call(
        kernel,
        out_shape=jax.ShapeDtypeStruct(queries.shape, BF16),
        in_specs=[pl.BlockSpec(memory_space=pltpu.SMEM), vmem, vmem, hbm, hbm, hbm, hbm],
        out_specs=hbm,
        scratch_shapes=[
            pltpu.VMEM((SEG, 3, C, C), BF16),
            pltpu.VMEM((SEG, 3, 16, C), BF16),
            pltpu.VMEM((SEG, 16, C), F32),
            pltpu.VMEM((SEG, 16, C), F32),
            square, square, square, square, square,
            pltpu.VMEM((2, C, C), F32),
            pltpu.VMEM((4, C, C), F32),
            pltpu.VMEM((C, C), F32),
            pltpu.VMEM((2, C, C), F32),
            pltpu.VMEM((SEG, C, C), BF16),
            dma((SEG, 4)), dma((SEG, 4)), dma((SEG, 3)), dma((SEG, 3)), dma((5,)), dma((4,)), dma((SEG,)), dma((SEG,)),
        ],
        compiler_params=pltpu.CompilerParams(
            collective_id=0, has_side_effects=True, vmem_limit_bytes=48 << 20
        ),
    )(doc_lengths, conv_weights, out_gain[None, :], scal, queries, keys, values_in)


def solution(mesh):
    in_specs = (
        P(("dp", "ctx"), None),
        P(("dp", "ctx"), None),
        P(("dp", "ctx"), None),
        P(),
        P(None, ("dp", "ctx")),
        P(None, ("dp", "ctx")),
        P(None, None, ("dp", "ctx")),
        P("dp"),
        P(),
    )
    out_specs = P(("dp", "ctx"), None)
    return jax.shard_map(body, mesh=mesh, in_specs=in_specs, out_specs=out_specs, check_vma=False)
```

```python
import functools
import jax
import jax.numpy as jnp
from jax import lax
from jax.experimental import pallas as pl
from jax.experimental.pallas import tpu as pltpu
from jax.sharding import PartitionSpec as P

F32 = jnp.float32
BF16 = jnp.bfloat16
C = 128
SEG = 16


def halves(x):
    high = x.astype(BF16)
    low = (x - high.astype(F32)).astype(BF16)
    return high, low


def left_form(x):
    return jnp.concatenate(halves(x), axis=1)


def twice(wide):
    return jnp.concatenate([wide, wide], axis=0)


def right_form(x):
    return twice(left_form(x))


def times(left, right):
    r = jnp.dot(left, right, preferred_element_type=F32)
    return r[:, :C] + r[:, C:]


def lanes_ds(i):
    return pl.ds(pl.multiple_of(i * C, C), C)


def fill_rows(first, doc_ref, msg_ref, rows_ref):
    bounds = []
    acc = jnp.int32(0)
    for i in range(doc_ref.shape[0]):
        bounds.append(acc)
        acc = acc + doc_ref[i]
    slab_pos = first + lax.broadcasted_iota(jnp.int32, (SEG, C), 0) * C
    pos = slab_pos + lax.broadcasted_iota(jnp.int32, (SEG, C), 1)

    def doc_of(p):
        total = jnp.zeros((SEG, C), F32)
        for b in bounds:
            total = total + jnp.where(p >= b, 1.0, 0.0)
        return total

    doc = doc_of(pos)
    upper = (lax.broadcasted_iota(jnp.int32, (C, C), 0) <= lax.broadcasted_iota(jnp.int32, (C, C), 1)).astype(F32)
    slabs = pl.ds(1, SEG)
    cum = jnp.dot(msg_ref[slabs, 0, :], upper, precision=lax.Precision.HIGHEST, preferred_element_type=F32)
    rows_ref[:, 0, :] = cum
    for r in range(1, 9):
        rows_ref[:, r, :] = msg_ref[slabs, r, :]
    rows_ref[:, 9, :] = doc
    rows_ref[:, 10, :] = jnp.where(doc == doc_of(slab_pos - 1), jnp.exp(cum), 0.0)
    for m in (1, 2, 3):
        rows_ref[:, 10 + m, :] = jnp.where(doc == doc_of(pos - m), 1.0, 0.0)
    rows_ref[:, 14, :] = jnp.zeros((SEG, C), F32)
    rows_ref[:, 15, :] = jnp.zeros((SEG, C), F32)


def conv(j, a, cols, taps_ref, x_ref, msg_ref):
    x = x_ref[j, a].astype(F32)
    before = msg_ref[j, 9 + 3 * a : 12 + 3 * a, :]
    total = taps_ref[a, 0:1, :] * x
    for m in (1, 2, 3):
        moved = jnp.concatenate([before[3 - m :], x[: C - m]], axis=0)
        total = total + taps_ref[a, m : m + 1, :] * moved * cols[:, 10 + m : 11 + m]
    return total / (1.0 + jnp.exp(-total))


def unit(x):
    return x * lax.rsqrt(jnp.sum(x * x, axis=1, keepdims=True) + 1e-06)


def slab_states(js, taps_ref, rows_ref, x_ref, msg_ref, kt_ref, inv_ref, v_ref, hk_ref, decay_ref, trans_ref, write_ref):
    above = lax.broadcasted_iota(jnp.int32, (C, C), 0)
    along = lax.broadcasted_iota(jnp.int32, (C, C), 1)
    lower = above >= along
    apart = jnp.where(above > along, above ^ along, 0)
    eye = jnp.where(above == along, 1.0, 0.0)
    n = len(js)
    k, cols, rows = [], [], []
    for j in js:
        r = rows_ref[j]
        c = r.T
        rows.append(r)
        cols.append(c)
        k.append(unit(conv(j, 1, c, taps_ref, x_ref, msg_ref)))
        v_ref[j] = left_form(conv(j, 2, c, taps_ref, x_ref, msg_ref))
    kt = [x.T for x in k]
    outer, system = [], []
    for i in range(n):
        wide = left_form(kt[i])
        kt_ref[js[i]] = wide
        r, c = rows[i], cols[i]
        gram = times(left_form(k[i]), twice(wide))
        hk_ref[js[i]] = left_form(k[i] * c[:, 10:11])
        keep = lower & (c[:, 9:10] == r[9:10])
        decay = jnp.exp(jnp.where(keep, c[:, 0:1] - r[0:1], -1e30)) * r[1:2]
        last = jnp.exp(jnp.where(keep[C - 1 : C], r[0:1, C - 1 : C] - r[0:1], -1e30)) * r[1:2]
        decay_ref[js[i]] = decay
        outer.append(kt[i] * last)
        system.append(decay * gram)
    inverse = [eye - jnp.where(apart == 1, system[i], 0.0) for i in range(n)]
    b = 2
    while b < C:
        pick = (apart >= b) & (apart < 2 * b)
        half = [times(left_form(inverse[i]), right_form(jnp.where(pick, system[i], 0.0))) for i in range(n)]
        inverse = [inverse[i] - times(left_form(half[i]), right_form(inverse[i])) for i in range(n)]
        b *= 2
    wide = [left_form(inverse[i]) for i in range(n)]
    for i in range(n):
        inv_ref[js[i]] = wide[i]
    mixed = [left_form(times(left_form(outer[i]), twice(wide[i]))) for i in range(n)]
    for i in range(n):
        write_ref[js[i]] = times(mixed[i], twice(v_ref[js[i]]))
        trans_ref[js[i]] = rows[i][10:11, C - 1 : C] * eye - times(mixed[i], twice(hk_ref[js[i]]))


def block_totals(trans_ref, write_ref, lev_ref, seg_ref):
    blocks = [(trans_ref[j], write_ref[j]) for j in range(SEG)]
    kept = 0
    while len(blocks) > 1:
        joined = []
        for a in range(0, len(blocks), 2):
            upper = left_form(blocks[a + 1][0])
            lower = [left_form(x) for x in blocks[a]]
            for part in (0, 1):
                lev_ref[kept, part] = lower[part]
            kept += 1
            joined.append((times(upper, twice(lower[0])), times(upper, twice(lower[1])) + blocks[a + 1][1]))
        blocks = joined
    seg_ref[0] = blocks[0][0]
    seg_ref[1] = blocks[0][1]


def level_reads(rows_ref, lev_ref, local_ref, reach_ref):
    kept = 0
    for level in range(1, 5):
        size = 1 << (level - 1)
        for first in range(size, SEG, 2 * size):
            at = pl.ds(first * C, size * C)
            reach = reach_ref[at, :]
            got = times(reach, twice(lev_ref[kept, 1]))
            for d in range(size):
                weight = rows_ref[first + d].T[:, 2 + level : 3 + level]
                local_ref[first + d] = local_ref[first + d] + got[d * C : (d + 1) * C] * weight
            reach_ref[at, :] = left_form(times(reach, twice(lev_ref[kept, 0])))
            kept += 1


def slab_reads(js, taps_ref, rows_ref, x_ref, msg_ref, kt_ref, inv_ref, v_ref, hk_ref, decay_ref, local_ref, reach_ref):
    n = len(js)
    q, cols = [], []
    for j in js:
        c = rows_ref[j].T
        cols.append(c)
        q.append(unit(conv(j, 0, c, taps_ref, x_ref, msg_ref)) * C ** (-0.5))
    attn = [left_form(times(left_form(q[i]), twice(kt_ref[js[i]])) * decay_ref[js[i]]) for i in range(n)]
    attn = [left_form(times(attn[i], twice(inv_ref[js[i]]))) for i in range(n)]
    for i in range(n):
        local_ref[js[i]] = times(attn[i], twice(v_ref[js[i]])) * cols[i][:, 2:3]
        qeff = q[i] * cols[i][:, 10:11] - times(attn[i], twice(hk_ref[js[i]]))
        reach_ref[pl.ds(pl.multiple_of(js[i] * C, C), C), :] = left_form(qeff)


def final(j, s5, s6, gain, rows_ref, local_ref, reach_ref):
    c = rows_ref[j].T
    reach = reach_ref[pl.ds(pl.multiple_of(j * C, C), C), :]
    o = local_ref[j] + times(reach, s5) * c[:, 7:8] + times(reach, s6) * c[:, 8:9]
    return (o * lax.rsqrt(jnp.mean(o * o, axis=1, keepdims=True) + 1e-06) * gain).astype(BF16)


def kernel(
    doc_src, cw_src, gain_src, gates_src, betas_src, weights_src, q_src, k_src, v_src, out_ref,
    doc_ref, taps_ref, gain_ref, raw_ref, tail_ref, pack_ref, msg_ref, x_ref, rows_ref,
    kt_ref, inv_ref, v_ref, hk_ref, decay_ref, trans_ref, write_ref, lev_ref, local_ref, reach_ref,
    seg_ref, far_ref, joint_ref, states_ref, stage_ref,
    load_sem, msg_send, msg_recv, edge_send, in_send, in_recv, far_send, far_recv, out_send, out_recv,
):
    me = lax.axis_index("ctx")
    segment = lax.div(me, SEG)
    mine = lax.rem(me, SEG)
    my_z, my_x, my_core = lax.div(mine, 8), lax.rem(lax.div(mine, 2), 4), lax.rem(mine, 2)
    sources = (q_src, k_src, v_src)

    loads = [
        pltpu.make_async_copy(gates_src, raw_ref.at[0], load_sem.at[0]),
        pltpu.make_async_copy(betas_src, raw_ref.at[1], load_sem.at[1]),
        pltpu.make_async_copy(weights_src, raw_ref.at[pl.ds(2, 7)], load_sem.at[2]),
    ]
    loads += [
        pltpu.make_async_copy(sources[a].at[pl.ds(C - 16, 16), :], tail_ref.at[a], load_sem.at[3 + a]) for a in range(3)
    ]
    small = [
        pltpu.make_async_copy(cw_src.at[:, lanes_ds(SEG * a + mine)], taps_ref.at[a], load_sem.at[6 + a]) for a in range(3)
    ]
    small += [
        pltpu.make_async_copy(gain_src.at[:, lanes_ds(mine)], gain_ref, load_sem.at[9]),
        pltpu.make_async_copy(doc_src, doc_ref, load_sem.at[10]),
    ]
    for copy in loads + small:
        copy.start()

    def place(dz, dx, dc):
        return lax.rem(my_z + dz, 2) * 8 + lax.rem(my_x + dx, 4) * 2 + lax.rem(my_core + dc, 2)

    def at(seg, head):
        return {"ctx": lax.rem(seg, 4) * SEG + head}

    barrier = pltpu.get_barrier_semaphore()

    def greet(target):
        pl.semaphore_signal(barrier, inc=1, device_id=target, device_id_type=pl.DeviceIdType.MESH)

    for n in range(1, 4):
        greet(at(segment + n, mine))
    greet(at(segment + 3, SEG - 1))
    for n in range(1, SEG):
        greet(at(segment, lax.rem(mine + n, SEG)))

    @pl.when(mine == SEG - 1)
    def _():
        for n in range(SEG):
            greet(at(segment + 1, n))

    def keeping(a):
        return pltpu.make_async_copy(sources[a].at[:, lanes_ds(mine)], x_ref.at[mine, a], in_recv.at[mine, a])

    for a in (1, 2, 0):
        keeping(a).start()
    for copy in loads:
        copy.wait()
    for r in range(9):
        pack_ref[:, r, :] = raw_ref[r]
    for h in range(SEG):
        for a in range(3):
            pack_ref[h, 9 + 3 * a : 12 + 3 * a, :] = tail_ref[a, 8:16, h * C : (h + 1) * C].astype(F32)[5:8]
    for r in range(18, 24):
        pack_ref[:, r, :] = jnp.zeros((SEG, C), F32)

    @pl.when(mine == SEG - 1)
    def _():
        pl.semaphore_wait(barrier, 19 + SEG)

    @pl.when(mine != SEG - 1)
    def _():
        pl.semaphore_wait(barrier, 19)

    order = [(dz, dx, dc) for dx in (0, 1, 3, 2) for dz in (0, 1) for dc in (0, 1)][1:]

    def message(head):
        return pltpu.make_async_remote_copy(
            src_ref=pack_ref.at[head], dst_ref=msg_ref.at[mine + 1],
            send_sem=msg_send.at[head], recv_sem=msg_recv.at[mine + 1],
            device_id=at(segment, head), device_id_type=pl.DeviceIdType.MESH,
        )

    def message_from(slab):
        return pltpu.make_async_remote_copy(
            src_ref=pack_ref.at[slab], dst_ref=msg_ref.at[slab + 1],
            send_sem=msg_send.at[slab], recv_sem=msg_recv.at[slab + 1],
            device_id=at(segment, slab), device_id_type=pl.DeviceIdType.MESH,
        )

    own_message = pltpu.make_async_copy(pack_ref.at[mine], msg_ref.at[mine + 1], msg_recv.at[mine + 1])

    def edge(head):
        return pltpu.make_async_remote_copy(
            src_ref=pack_ref.at[head], dst_ref=msg_ref.at[0],
            send_sem=edge_send.at[head], recv_sem=msg_recv.at[0],
            device_id=at(segment + 1, head), device_id_type=pl.DeviceIdType.MESH,
        )

    def sending(a, head):
        return pltpu.make_async_remote_copy(
            src_ref=sources[a].at[:, lanes_ds(head)], dst_ref=x_ref.at[mine, a],
            send_sem=in_send.at[head, a], recv_sem=in_recv.at[mine, a],
            device_id=at(segment, head), device_id_type=pl.DeviceIdType.MESH,
        )

    def arriving(a, slab):
        return pltpu.make_async_remote_copy(
            src_ref=sources[a].at[:, lanes_ds(slab)], dst_ref=x_ref.at[slab, a],
            send_sem=in_send.at[slab, a], recv_sem=in_recv.at[slab, a],
            device_id=at(segment, slab), device_id_type=pl.DeviceIdType.MESH,
        )

    own_message.start()
    for step in order:
        message(place(*step)).start()

    @pl.when(mine == SEG - 1)
    def _():
        for n in range(SEG):
            edge(jnp.int32(n)).start()

    for step in order:
        for a in (1, 2):
            sending(a, place(*step)).start()
    for step in order:
        sending(0, place(*step)).start()

    for copy in small:
        copy.wait()
    own_message.wait()
    for step in order:
        message_from(place(*step)).wait_recv()
    edge(mine).wait_recv()
    fill_rows(segment * (SEG * C), doc_ref, msg_ref, rows_ref)

    def members(m):
        dx = m + lax.div(m, 2) - 2 * lax.div(m, 3)
        x = lax.rem(my_x + 4 - dx, 4)
        return [z * 8 + x * 2 + core for z in (0, 1) for core in (0, 1)]

    def await_inputs(js, arrays):
        for j in js:
            @pl.when(j == mine)
            def _():
                for a in arrays:
                    keeping(a).wait()

            @pl.when(j != mine)
            def _():
                for a in arrays:
                    arriving(a, j).wait_recv()

    def state_group(m, _):
        js = members(m)
        await_inputs(js, (1, 2))
        slab_states(
            js, taps_ref, rows_ref, x_ref, msg_ref, kt_ref, inv_ref, v_ref, hk_ref, decay_ref, trans_ref, write_ref
        )
        return 0

    lax.fori_loop(0, 4, state_group, 0)

    def across(n, src, to, slot):
        return pltpu.make_async_remote_copy(
            src_ref=src, dst_ref=far_ref.at[slot], send_sem=far_send.at[n], recv_sem=far_recv.at[slot],
            device_id=at(jnp.int32(to), mine), device_id_type=pl.DeviceIdType.MESH,
        )

    block_totals(trans_ref, write_ref, lev_ref, seg_ref)
    first_write = across(0, seg_ref.at[1], 1, 0)
    third_trans = across(1, seg_ref.at[0], 3, 1)
    third_write = across(2, seg_ref.at[1], 3, 2)
    to_third = across(3, joint_ref, 2, 3)
    to_fourth = across(4, joint_ref, 3, 3)

    @pl.when(segment == 0)
    def _():
        first_write.start()

    @pl.when(segment == 2)
    def _():
        third_trans.start()
        third_write.start()

    states_ref[...] = jnp.zeros_like(states_ref)

    def read_group(m, _):
        @pl.when((segment == 1) & (m == 3))
        def _():
            first_write.wait_recv()
            states_ref[0] = far_ref[0]
            joint_ref[...] = times(left_form(seg_ref[0]), right_form(far_ref[0])) + seg_ref[1]
            to_fourth.start()
            to_third.start()

        js = members(m)
        await_inputs(js, (0,))
        slab_reads(
            js, taps_ref, rows_ref, x_ref, msg_ref,
            kt_ref, inv_ref, v_ref, hk_ref, decay_ref, local_ref, reach_ref,
        )
        return 0

    lax.fori_loop(0, 4, read_group, 0)
    level_reads(rows_ref, lev_ref, local_ref, reach_ref)

    @pl.when(segment == 2)
    def _():
        to_third.wait_recv()
        states_ref[1] = far_ref[3]

    @pl.when(segment == 3)
    def _():
        third_trans.wait_recv()
        third_write.wait_recv()
        states_ref[0] = far_ref[2]
        to_fourth.wait_recv()
        states_ref[1] = times(left_form(far_ref[1]), right_form(far_ref[3]))

    gain = gain_ref[...]
    s5 = right_form(states_ref[0])
    s6 = right_form(states_ref[1])

    def leaving(slab):
        return pltpu.make_async_remote_copy(
            src_ref=stage_ref.at[slab], dst_ref=out_ref.at[:, lanes_ds(mine)],
            send_sem=out_send.at[slab], recv_sem=out_recv.at[mine],
            device_id=at(segment, slab), device_id_type=pl.DeviceIdType.MESH,
        )

    def returning(head):
        return pltpu.make_async_remote_copy(
            src_ref=stage_ref.at[head], dst_ref=out_ref.at[:, lanes_ds(head)],
            send_sem=out_send.at[head], recv_sem=out_recv.at[head],
            device_id=at(segment, head), device_id_type=pl.DeviceIdType.MESH,
        )

    for dx in (2, 1, 3, 0):
        js = [place(dz, dx, dc) for dz in (1, 0) for dc in (1, 0)]
        for j in js:
            stage_ref[j] = final(j, s5, s6, gain, rows_ref, local_ref, reach_ref)
        for j in js[: 4 if dx else 3]:
            leaving(j).start()
    home = pltpu.make_async_copy(stage_ref.at[mine], out_ref.at[:, lanes_ds(mine)], out_recv.at[mine])
    home.start()
    home.wait()
    for step in order:
        returning(place(*step)).wait_recv()

    for step in order:
        head = place(*step)
        message(head).wait_send()
        for a in range(3):
            sending(a, head).wait_send()
        leaving(head).wait_send()

    @pl.when(mine == SEG - 1)
    def _():
        for n in range(SEG):
            edge(jnp.int32(n)).wait_send()

    @pl.when(segment == 0)
    def _():
        first_write.wait_send()

    @pl.when(segment == 1)
    def _():
        to_third.wait_send()
        to_fourth.wait_send()

    @pl.when(segment == 2)
    def _():
        third_trans.wait_send()
        third_write.wait_send()


def body(queries, keys, values_in, conv_weights, log_gates, betas, level_weights, doc_lengths, out_gain):
    square = pltpu.VMEM((SEG, C, C), F32)
    wide = pltpu.VMEM((SEG, C, 2 * C), BF16)
    hbm = pl.BlockSpec(memory_space=pl.ANY)
    dma = pltpu.SemaphoreType.DMA
    return pl.pallas_call(
        kernel,
        out_shape=jax.ShapeDtypeStruct(queries.shape, BF16),
        in_specs=[hbm] * 9,
        out_specs=hbm,
        scratch_shapes=[
            pltpu.SMEM(doc_lengths.shape, jnp.int32),
            pltpu.VMEM((3, 4, C), F32),
            pltpu.VMEM((1, C), F32),
            pltpu.VMEM((9, SEG, C), F32),
            pltpu.VMEM((3, 16, queries.shape[1]), BF16),
            pltpu.VMEM((SEG, 24, C), F32),
            pltpu.VMEM((SEG + 1, 24, C), F32),
            pltpu.VMEM((SEG, 3, C, C), BF16),
            pltpu.VMEM((SEG, 16, C), F32),
            wide, wide, wide, wide, square, square, square,
            pltpu.VMEM((SEG - 1, 2, C, 2 * C), BF16),
            square,
            pltpu.VMEM((SEG * C, 2 * C), BF16),
            pltpu.VMEM((2, C, C), F32),
            pltpu.VMEM((4, C, C), F32),
            pltpu.VMEM((C, C), F32),
            pltpu.VMEM((2, C, C), F32),
            pltpu.VMEM((SEG, C, C), BF16),
            dma((11,)), dma((SEG,)), dma((SEG + 1,)), dma((SEG,)), dma((SEG, 3)), dma((SEG, 3)),
            dma((5,)), dma((4,)), dma((SEG,)), dma((SEG,)),
        ],
        compiler_params=pltpu.CompilerParams(
            collective_id=0, has_side_effects=True, vmem_limit_bytes=60 << 20
        ),
    )(
        doc_lengths, conv_weights, out_gain[None, :], log_gates, betas, level_weights, queries, keys, values_in
    )


def solution(mesh):
    in_specs = (
        P(("dp", "ctx"), None),
        P(("dp", "ctx"), None),
        P(("dp", "ctx"), None),
        P(),
        P(None, ("dp", "ctx")),
        P(None, ("dp", "ctx")),
        P(None, None, ("dp", "ctx")),
        P("dp"),
        P(),
    )
    out_specs = P(("dp", "ctx"), None)
    return jax.shard_map(body, mesh=mesh, in_specs=in_specs, out_specs=out_specs, check_vma=False)
```

```python
import functools
import jax
import jax.numpy as jnp
from jax import lax
from jax.experimental import pallas as pl
from jax.experimental.pallas import tpu as pltpu
from jax.sharding import PartitionSpec as P

F32 = jnp.float32
BF16 = jnp.bfloat16
C = 128
SEG = 16


def halves(x):
    high = x.astype(BF16)
    low = (x - high.astype(F32)).astype(BF16)
    return high, low


def left_form(x):
    return jnp.concatenate(halves(x), axis=1)


def twice(wide):
    return jnp.concatenate([wide, wide], axis=0)


def right_form(x):
    return twice(left_form(x))


def times(left, right):
    r = jnp.dot(left, right, preferred_element_type=F32)
    return r[:, :C] + r[:, C:]


def lanes_ds(i):
    return pl.ds(pl.multiple_of(i * C, C), C)


def fill_rows(first, doc_ref, msg_ref, rows_ref):
    bounds = []
    acc = jnp.int32(0)
    for i in range(doc_ref.shape[0]):
        bounds.append(acc)
        acc = acc + doc_ref[i]
    slab_pos = first + lax.broadcasted_iota(jnp.int32, (SEG, C), 0) * C
    pos = slab_pos + lax.broadcasted_iota(jnp.int32, (SEG, C), 1)

    def doc_of(p):
        total = jnp.zeros((SEG, C), F32)
        for b in bounds:
            total = total + jnp.where(p >= b, 1.0, 0.0)
        return total

    doc = doc_of(pos)
    upper = (lax.broadcasted_iota(jnp.int32, (C, C), 0) <= lax.broadcasted_iota(jnp.int32, (C, C), 1)).astype(F32)
    slabs = pl.ds(1, SEG)
    cum = jnp.dot(msg_ref[slabs, 0, :], upper, precision=lax.Precision.HIGHEST, preferred_element_type=F32)
    rows_ref[:, 0, :] = cum
    for r in range(1, 9):
        rows_ref[:, r, :] = msg_ref[slabs, r, :]
    rows_ref[:, 9, :] = doc
    rows_ref[:, 10, :] = jnp.where(doc == doc_of(slab_pos - 1), jnp.exp(cum), 0.0)
    for m in (1, 2, 3):
        rows_ref[:, 10 + m, :] = jnp.where(doc == doc_of(pos - m), 1.0, 0.0)
    rows_ref[:, 14, :] = jnp.zeros((SEG, C), F32)
    rows_ref[:, 15, :] = jnp.zeros((SEG, C), F32)


def conv(j, a, cols, taps_ref, x_ref, msg_ref):
    x = x_ref[j, a].astype(F32)
    before = msg_ref[j, 9 + 3 * a : 12 + 3 * a, :]
    total = taps_ref[a, 0:1, :] * x
    for m in (1, 2, 3):
        moved = jnp.concatenate([before[3 - m :], x[: C - m]], axis=0)
        total = total + taps_ref[a, m : m + 1, :] * moved * cols[:, 10 + m : 11 + m]
    return total / (1.0 + jnp.exp(-total))


def unit(x):
    return x * lax.rsqrt(jnp.sum(x * x, axis=1, keepdims=True) + 1e-06)


def slab_states(js, taps_ref, rows_ref, x_ref, msg_ref, kt_ref, inv_ref, v_ref, hk_ref, decay_ref, trans_ref, write_ref):
    above = lax.broadcasted_iota(jnp.int32, (C, C), 0)
    along = lax.broadcasted_iota(jnp.int32, (C, C), 1)
    lower = above >= along
    apart = jnp.where(above > along, above ^ along, 0)
    eye = jnp.where(above == along, 1.0, 0.0)
    n = len(js)
    k, cols, rows = [], [], []
    for j in js:
        r = rows_ref[j]
        c = r.T
        rows.append(r)
        cols.append(c)
        k.append(unit(conv(j, 1, c, taps_ref, x_ref, msg_ref)))
        v_ref[j] = left_form(conv(j, 2, c, taps_ref, x_ref, msg_ref))
    kt = [x.T for x in k]
    outer, system = [], []
    for i in range(n):
        wide = left_form(kt[i])
        kt_ref[js[i]] = wide
        r, c = rows[i], cols[i]
        gram = times(left_form(k[i]), twice(wide))
        hk_ref[js[i]] = left_form(k[i] * c[:, 10:11])
        keep = lower & (c[:, 9:10] == r[9:10])
        decay = jnp.exp(jnp.where(keep, c[:, 0:1] - r[0:1], -1e30)) * r[1:2]
        last = jnp.exp(jnp.where(keep[C - 1 : C], r[0:1, C - 1 : C] - r[0:1], -1e30)) * r[1:2]
        decay_ref[js[i]] = decay
        outer.append(kt[i] * last)
        system.append(decay * gram)
    inverse = [eye - jnp.where(apart == 1, system[i], 0.0) for i in range(n)]
    b = 2
    while b < C:
        pick = (apart >= b) & (apart < 2 * b)
        half = [times(left_form(inverse[i]), right_form(jnp.where(pick, system[i], 0.0))) for i in range(n)]
        inverse = [inverse[i] - times(left_form(half[i]), right_form(inverse[i])) for i in range(n)]
        b *= 2
    wide = [left_form(inverse[i]) for i in range(n)]
    for i in range(n):
        inv_ref[js[i]] = wide[i]
    mixed = [left_form(times(left_form(outer[i]), twice(wide[i]))) for i in range(n)]
    for i in range(n):
        write_ref[js[i]] = times(mixed[i], twice(v_ref[js[i]]))
        trans_ref[js[i]] = rows[i][10:11, C - 1 : C] * eye - times(mixed[i], twice(hk_ref[js[i]]))


def block_totals(trans_ref, write_ref, lev_ref, seg_ref):
    blocks = [(trans_ref[j], write_ref[j]) for j in range(SEG)]
    kept = 0
    while len(blocks) > 1:
        joined = []
        for a in range(0, len(blocks), 2):
            upper = left_form(blocks[a + 1][0])
            lower = [left_form(x) for x in blocks[a]]
            for part in (0, 1):
                lev_ref[kept, part] = lower[part]
            kept += 1
            joined.append((times(upper, twice(lower[0])), times(upper, twice(lower[1])) + blocks[a + 1][1]))
        blocks = joined
    seg_ref[0] = blocks[0][0]
    seg_ref[1] = blocks[0][1]


def level_reads(rows_ref, lev_ref, local_ref, reach_ref):
    kept = 0
    for level in range(1, 5):
        size = 1 << (level - 1)
        for first in range(size, SEG, 2 * size):
            at = pl.ds(first * C, size * C)
            reach = reach_ref[at, :]
            got = times(reach, twice(lev_ref[kept, 1]))
            for d in range(size):
                weight = rows_ref[first + d].T[:, 2 + level : 3 + level]
                local_ref[first + d] = local_ref[first + d] + got[d * C : (d + 1) * C] * weight
            reach_ref[at, :] = left_form(times(reach, twice(lev_ref[kept, 0])))
            kept += 1


def slab_reads(js, taps_ref, rows_ref, x_ref, msg_ref, kt_ref, inv_ref, v_ref, hk_ref, decay_ref, local_ref, reach_ref):
    n = len(js)
    q, cols = [], []
    for j in js:
        c = rows_ref[j].T
        cols.append(c)
        q.append(unit(conv(j, 0, c, taps_ref, x_ref, msg_ref)) * C ** (-0.5))
    attn = [left_form(times(left_form(q[i]), twice(kt_ref[js[i]])) * decay_ref[js[i]]) for i in range(n)]
    attn = [left_form(times(attn[i], twice(inv_ref[js[i]]))) for i in range(n)]
    for i in range(n):
        local_ref[js[i]] = times(attn[i], twice(v_ref[js[i]])) * cols[i][:, 2:3]
        qeff = q[i] * cols[i][:, 10:11] - times(attn[i], twice(hk_ref[js[i]]))
        reach_ref[pl.ds(pl.multiple_of(js[i] * C, C), C), :] = left_form(qeff)


def final(j, s5, s6, gain, rows_ref, local_ref, reach_ref):
    c = rows_ref[j].T
    reach = reach_ref[pl.ds(pl.multiple_of(j * C, C), C), :]
    o = local_ref[j] + times(reach, s5) * c[:, 7:8] + times(reach, s6) * c[:, 8:9]
    return (o * lax.rsqrt(jnp.mean(o * o, axis=1, keepdims=True) + 1e-06) * gain).astype(BF16)


def kernel(
    doc_src, cw_src, gain_src, gates_src, betas_src, weights_src, q_src, k_src, v_src, out_ref,
    doc_ref, taps_ref, gain_ref, raw_ref, tail_ref, pack_ref, msg_ref, x_ref, rows_ref,
    kt_ref, inv_ref, v_ref, hk_ref, decay_ref, trans_ref, write_ref, lev_ref, local_ref, reach_ref,
    seg_ref, far_ref, joint_ref, states_ref, stage_ref,
    load_sem, msg_send, msg_recv, edge_send, in_send, in_recv, far_send, far_recv, out_send, out_recv,
):
    me = lax.axis_index("ctx")
    segment = lax.div(me, SEG)
    mine = lax.rem(me, SEG)
    my_z, my_x, my_core = lax.div(mine, 8), lax.rem(lax.div(mine, 2), 4), lax.rem(mine, 2)
    sources = (q_src, k_src, v_src)

    loads = [
        pltpu.make_async_copy(gates_src, raw_ref.at[0], load_sem.at[0]),
        pltpu.make_async_copy(betas_src, raw_ref.at[1], load_sem.at[1]),
        pltpu.make_async_copy(weights_src, raw_ref.at[pl.ds(2, 7)], load_sem.at[2]),
    ]
    loads += [
        pltpu.make_async_copy(sources[a].at[pl.ds(C - 16, 16), :], tail_ref.at[a], load_sem.at[3 + a]) for a in range(3)
    ]
    small = [
        pltpu.make_async_copy(cw_src.at[:, lanes_ds(SEG * a + mine)], taps_ref.at[a], load_sem.at[6 + a]) for a in range(3)
    ]
    small += [
        pltpu.make_async_copy(gain_src.at[:, lanes_ds(mine)], gain_ref, load_sem.at[9]),
        pltpu.make_async_copy(doc_src, doc_ref, load_sem.at[10]),
    ]
    for copy in loads + small:
        copy.start()

    def place(dz, dx, dc):
        return lax.rem(my_z + dz, 2) * 8 + lax.rem(my_x + dx, 4) * 2 + lax.rem(my_core + dc, 2)

    def at(seg, head):
        return {"ctx": lax.rem(seg, 4) * SEG + head}

    barrier = pltpu.get_barrier_semaphore()

    def greet(target):
        pl.semaphore_signal(barrier, inc=1, device_id=target, device_id_type=pl.DeviceIdType.MESH)

    for n in range(1, 4):
        greet(at(segment + n, mine))
    greet(at(segment + 3, SEG - 1))
    for n in range(1, SEG):
        greet(at(segment, lax.rem(mine + n, SEG)))

    @pl.when(mine == SEG - 1)
    def _():
        for n in range(SEG):
            greet(at(segment + 1, n))

    def keeping(a):
        return pltpu.make_async_copy(sources[a].at[:, lanes_ds(mine)], x_ref.at[mine, a], in_recv.at[mine, a])

    for a in (1, 2, 0):
        keeping(a).start()
    for copy in loads:
        copy.wait()
    for r in range(9):
        pack_ref[:, r, :] = raw_ref[r]
    for h in range(SEG):
        for a in range(3):
            pack_ref[h, 9 + 3 * a : 12 + 3 * a, :] = tail_ref[a, 8:16, h * C : (h + 1) * C].astype(F32)[5:8]
    for r in range(18, 24):
        pack_ref[:, r, :] = jnp.zeros((SEG, C), F32)

    @pl.when(mine == SEG - 1)
    def _():
        pl.semaphore_wait(barrier, 19 + SEG)

    @pl.when(mine != SEG - 1)
    def _():
        pl.semaphore_wait(barrier, 19)

    order = [(dz, dx, dc) for dx in (0, 1, 3, 2) for dz in (0, 1) for dc in (0, 1)][1:]

    def message(head):
        return pltpu.make_async_remote_copy(
            src_ref=pack_ref.at[head], dst_ref=msg_ref.at[mine + 1],
            send_sem=msg_send.at[head], recv_sem=msg_recv.at[mine + 1],
            device_id=at(segment, head), device_id_type=pl.DeviceIdType.MESH,
        )

    def message_from(slab):
        return pltpu.make_async_remote_copy(
            src_ref=pack_ref.at[slab], dst_ref=msg_ref.at[slab + 1],
            send_sem=msg_send.at[slab], recv_sem=msg_recv.at[slab + 1],
            device_id=at(segment, slab), device_id_type=pl.DeviceIdType.MESH,
        )

    own_message = pltpu.make_async_copy(pack_ref.at[mine], msg_ref.at[mine + 1], msg_recv.at[mine + 1])

    def edge(head):
        return pltpu.make_async_remote_copy(
            src_ref=pack_ref.at[head], dst_ref=msg_ref.at[0],
            send_sem=edge_send.at[head], recv_sem=msg_recv.at[0],
            device_id=at(segment + 1, head), device_id_type=pl.DeviceIdType.MESH,
        )

    def sending(a, head):
        return pltpu.make_async_remote_copy(
            src_ref=sources[a].at[:, lanes_ds(head)], dst_ref=x_ref.at[mine, a],
            send_sem=in_send.at[head, a], recv_sem=in_recv.at[mine, a],
            device_id=at(segment, head), device_id_type=pl.DeviceIdType.MESH,
        )

    def arriving(a, slab):
        return pltpu.make_async_remote_copy(
            src_ref=sources[a].at[:, lanes_ds(slab)], dst_ref=x_ref.at[slab, a],
            send_sem=in_send.at[slab, a], recv_sem=in_recv.at[slab, a],
            device_id=at(segment, slab), device_id_type=pl.DeviceIdType.MESH,
        )

    own_message.start()
    for step in order:
        message(place(*step)).start()

    @pl.when(mine == SEG - 1)
    def _():
        for n in range(SEG):
            edge(jnp.int32(n)).start()

    for step in order:
        for a in (1, 2):
            sending(a, place(*step)).start()
    for step in order:
        sending(0, place(*step)).start()

    for copy in small:
        copy.wait()
    own_message.wait()
    for step in order:
        message_from(place(*step)).wait_recv()
    edge(mine).wait_recv()
    fill_rows(segment * (SEG * C), doc_ref, msg_ref, rows_ref)

    def members(m):
        dx = m + lax.div(m, 2) - 2 * lax.div(m, 3)
        x = lax.rem(my_x + 4 - dx, 4)
        return [z * 8 + x * 2 + core for z in (0, 1) for core in (0, 1)]

    def await_inputs(js, arrays):
        for j in js:
            @pl.when(j == mine)
            def _():
                for a in arrays:
                    keeping(a).wait()

            @pl.when(j != mine)
            def _():
                for a in arrays:
                    arriving(a, j).wait_recv()

    def state_group(m, _):
        js = members(2 * m) + members(2 * m + 1)
        await_inputs(js, (1, 2))
        slab_states(
            js, taps_ref, rows_ref, x_ref, msg_ref, kt_ref, inv_ref, v_ref, hk_ref, decay_ref, trans_ref, write_ref
        )
        return 0

    lax.fori_loop(0, 2, state_group, 0)

    def across(n, src, to, slot):
        return pltpu.make_async_remote_copy(
            src_ref=src, dst_ref=far_ref.at[slot], send_sem=far_send.at[n], recv_sem=far_recv.at[slot],
            device_id=at(jnp.int32(to), mine), device_id_type=pl.DeviceIdType.MESH,
        )

    block_totals(trans_ref, write_ref, lev_ref, seg_ref)
    first_write = across(0, seg_ref.at[1], 1, 0)
    third_trans = across(1, seg_ref.at[0], 3, 1)
    third_write = across(2, seg_ref.at[1], 3, 2)
    to_third = across(3, joint_ref, 2, 3)
    to_fourth = across(4, joint_ref, 3, 3)

    @pl.when(segment == 0)
    def _():
        first_write.start()

    @pl.when(segment == 2)
    def _():
        third_trans.start()
        third_write.start()

    states_ref[...] = jnp.zeros_like(states_ref)

    def read_group(m, _):
        @pl.when((segment == 1) & (m == 1))
        def _():
            first_write.wait_recv()
            states_ref[0] = far_ref[0]
            joint_ref[...] = times(left_form(seg_ref[0]), right_form(far_ref[0])) + seg_ref[1]
            to_fourth.start()
            to_third.start()

        js = members(2 * m) + members(2 * m + 1)
        await_inputs(js, (0,))
        slab_reads(
            js, taps_ref, rows_ref, x_ref, msg_ref,
            kt_ref, inv_ref, v_ref, hk_ref, decay_ref, local_ref, reach_ref,
        )
        return 0

    lax.fori_loop(0, 2, read_group, 0)
    level_reads(rows_ref, lev_ref, local_ref, reach_ref)

    @pl.when(segment == 2)
    def _():
        to_third.wait_recv()
        states_ref[1] = far_ref[3]

    @pl.when(segment == 3)
    def _():
        third_trans.wait_recv()
        third_write.wait_recv()
        states_ref[0] = far_ref[2]
        to_fourth.wait_recv()
        states_ref[1] = times(left_form(far_ref[1]), right_form(far_ref[3]))

    gain = gain_ref[...]
    s5 = right_form(states_ref[0])
    s6 = right_form(states_ref[1])

    def leaving(slab):
        return pltpu.make_async_remote_copy(
            src_ref=stage_ref.at[slab], dst_ref=out_ref.at[:, lanes_ds(mine)],
            send_sem=out_send.at[slab], recv_sem=out_recv.at[mine],
            device_id=at(segment, slab), device_id_type=pl.DeviceIdType.MESH,
        )

    def returning(head):
        return pltpu.make_async_remote_copy(
            src_ref=stage_ref.at[head], dst_ref=out_ref.at[:, lanes_ds(head)],
            send_sem=out_send.at[head], recv_sem=out_recv.at[head],
            device_id=at(segment, head), device_id_type=pl.DeviceIdType.MESH,
        )

    for dx in (2, 1, 3, 0):
        js = [place(dz, dx, dc) for dz in (1, 0) for dc in (1, 0)]
        for j in js:
            stage_ref[j] = final(j, s5, s6, gain, rows_ref, local_ref, reach_ref)
        for j in js[: 4 if dx else 3]:
            leaving(j).start()
    home = pltpu.make_async_copy(stage_ref.at[mine], out_ref.at[:, lanes_ds(mine)], out_recv.at[mine])
    home.start()
    home.wait()
    for step in order:
        returning(place(*step)).wait_recv()

    for step in order:
        head = place(*step)
        message(head).wait_send()
        for a in range(3):
            sending(a, head).wait_send()
        leaving(head).wait_send()

    @pl.when(mine == SEG - 1)
    def _():
        for n in range(SEG):
            edge(jnp.int32(n)).wait_send()

    @pl.when(segment == 0)
    def _():
        first_write.wait_send()

    @pl.when(segment == 1)
    def _():
        to_third.wait_send()
        to_fourth.wait_send()

    @pl.when(segment == 2)
    def _():
        third_trans.wait_send()
        third_write.wait_send()


def body(queries, keys, values_in, conv_weights, log_gates, betas, level_weights, doc_lengths, out_gain):
    square = pltpu.VMEM((SEG, C, C), F32)
    wide = pltpu.VMEM((SEG, C, 2 * C), BF16)
    hbm = pl.BlockSpec(memory_space=pl.ANY)
    dma = pltpu.SemaphoreType.DMA
    return pl.pallas_call(
        kernel,
        out_shape=jax.ShapeDtypeStruct(queries.shape, BF16),
        in_specs=[hbm] * 9,
        out_specs=hbm,
        scratch_shapes=[
            pltpu.SMEM(doc_lengths.shape, jnp.int32),
            pltpu.VMEM((3, 4, C), F32),
            pltpu.VMEM((1, C), F32),
            pltpu.VMEM((9, SEG, C), F32),
            pltpu.VMEM((3, 16, queries.shape[1]), BF16),
            pltpu.VMEM((SEG, 24, C), F32),
            pltpu.VMEM((SEG + 1, 24, C), F32),
            pltpu.VMEM((SEG, 3, C, C), BF16),
            pltpu.VMEM((SEG, 16, C), F32),
            wide, wide, wide, wide, square, square, square,
            pltpu.VMEM((SEG - 1, 2, C, 2 * C), BF16),
            square,
            pltpu.VMEM((SEG * C, 2 * C), BF16),
            pltpu.VMEM((2, C, C), F32),
            pltpu.VMEM((4, C, C), F32),
            pltpu.VMEM((C, C), F32),
            pltpu.VMEM((2, C, C), F32),
            pltpu.VMEM((SEG, C, C), BF16),
            dma((11,)), dma((SEG,)), dma((SEG + 1,)), dma((SEG,)), dma((SEG, 3)), dma((SEG, 3)),
            dma((5,)), dma((4,)), dma((SEG,)), dma((SEG,)),
        ],
        compiler_params=pltpu.CompilerParams(
            collective_id=0, has_side_effects=True, vmem_limit_bytes=60 << 20
        ),
    )(
        doc_lengths, conv_weights, out_gain[None, :], log_gates, betas, level_weights, queries, keys, values_in
    )


def solution(mesh):
    in_specs = (
        P(("dp", "ctx"), None),
        P(("dp", "ctx"), None),
        P(("dp", "ctx"), None),
        P(),
        P(None, ("dp", "ctx")),
        P(None, ("dp", "ctx")),
        P(None, None, ("dp", "ctx")),
        P("dp"),
        P(),
    )
    out_specs = P(("dp", "ctx"), None)
    return jax.shard_map(body, mesh=mesh, in_specs=in_specs, out_specs=out_specs, check_vma=False)
```

```python
import functools
import jax
import jax.numpy as jnp
from jax import lax
from jax.experimental import pallas as pl
from jax.experimental.pallas import tpu as pltpu
from jax.sharding import PartitionSpec as P

F32 = jnp.float32
BF16 = jnp.bfloat16
C = 128
SEG = 16


def halves(x):
    high = x.astype(BF16)
    low = (x - high.astype(F32)).astype(BF16)
    return high, low


def left_form(x):
    return jnp.concatenate(halves(x), axis=1)


def twice(wide):
    return jnp.concatenate([wide, wide], axis=0)


def right_form(x):
    return twice(left_form(x))


def times(left, right):
    r = jnp.dot(left, right, preferred_element_type=F32)
    return r[:, :C] + r[:, C:]


def lanes_ds(i):
    return pl.ds(pl.multiple_of(i * C, C), C)


def fill_rows(first, doc_ref, msg_ref, rows_ref):
    bounds = []
    acc = jnp.int32(0)
    for i in range(doc_ref.shape[0]):
        bounds.append(acc)
        acc = acc + doc_ref[i]
    slab_pos = first + lax.broadcasted_iota(jnp.int32, (SEG, C), 0) * C
    pos = slab_pos + lax.broadcasted_iota(jnp.int32, (SEG, C), 1)

    def doc_of(p):
        total = jnp.zeros((SEG, C), F32)
        for b in bounds:
            total = total + jnp.where(p >= b, 1.0, 0.0)
        return total

    doc = doc_of(pos)
    upper = (lax.broadcasted_iota(jnp.int32, (C, C), 0) <= lax.broadcasted_iota(jnp.int32, (C, C), 1)).astype(F32)
    slabs = pl.ds(1, SEG)
    cum = jnp.dot(msg_ref[slabs, 0, :], upper, precision=lax.Precision.HIGHEST, preferred_element_type=F32)
    rows_ref[:, 0, :] = cum
    for r in range(1, 9):
        rows_ref[:, r, :] = msg_ref[slabs, r, :]
    rows_ref[:, 9, :] = doc
    rows_ref[:, 10, :] = jnp.where(doc == doc_of(slab_pos - 1), jnp.exp(cum), 0.0)
    for m in (1, 2, 3):
        rows_ref[:, 10 + m, :] = jnp.where(doc == doc_of(pos - m), 1.0, 0.0)
    rows_ref[:, 14, :] = jnp.zeros((SEG, C), F32)
    rows_ref[:, 15, :] = jnp.zeros((SEG, C), F32)


def conv(j, a, cols, taps_ref, x_ref, msg_ref):
    x = x_ref[j, a].astype(F32)
    before = msg_ref[j, 9 + 3 * a : 12 + 3 * a, :]
    total = taps_ref[a, 0:1, :] * x
    for m in (1, 2, 3):
        moved = jnp.concatenate([before[3 - m :], x[: C - m]], axis=0)
        total = total + taps_ref[a, m : m + 1, :] * moved * cols[:, 10 + m : 11 + m]
    return total / (1.0 + jnp.exp(-total))


def unit(x):
    return x * lax.rsqrt(jnp.sum(x * x, axis=1, keepdims=True) + 1e-06)


def slab_states(js, taps_ref, rows_ref, x_ref, msg_ref, kt_ref, inv_ref, v_ref, hk_ref, decay_ref, trans_ref, write_ref):
    above = lax.broadcasted_iota(jnp.int32, (C, C), 0)
    along = lax.broadcasted_iota(jnp.int32, (C, C), 1)
    lower = above >= along
    apart = jnp.where(above > along, above ^ along, 0)
    eye = jnp.where(above == along, 1.0, 0.0)
    n = len(js)
    k, cols, rows = [], [], []
    for j in js:
        r = rows_ref[j]
        c = r.T
        rows.append(r)
        cols.append(c)
        k.append(unit(conv(j, 1, c, taps_ref, x_ref, msg_ref)))
        v_ref[j] = left_form(conv(j, 2, c, taps_ref, x_ref, msg_ref))
    kt = [x.T for x in k]
    outer, system = [], []
    for i in range(n):
        wide = left_form(kt[i])
        kt_ref[js[i]] = wide
        r, c = rows[i], cols[i]
        gram = times(left_form(k[i]), twice(wide))
        hk_ref[js[i]] = left_form(k[i] * c[:, 10:11])
        keep = lower & (c[:, 9:10] == r[9:10])
        decay = jnp.exp(jnp.where(keep, c[:, 0:1] - r[0:1], -1e30)) * r[1:2]
        last = jnp.exp(jnp.where(keep[C - 1 : C], r[0:1, C - 1 : C] - r[0:1], -1e30)) * r[1:2]
        decay_ref[js[i]] = decay
        outer.append(kt[i] * last)
        system.append(decay * gram)
    inverse = [eye - jnp.where(apart == 1, system[i], 0.0) for i in range(n)]
    b = 2
    while b < C:
        pick = (apart >= b) & (apart < 2 * b)
        half = [times(left_form(inverse[i]), right_form(jnp.where(pick, system[i], 0.0))) for i in range(n)]
        inverse = [inverse[i] - times(left_form(half[i]), right_form(inverse[i])) for i in range(n)]
        b *= 2
    wide = [left_form(inverse[i]) for i in range(n)]
    for i in range(n):
        inv_ref[js[i]] = wide[i]
    mixed = [left_form(times(left_form(outer[i]), twice(wide[i]))) for i in range(n)]
    for i in range(n):
        write_ref[js[i]] = times(mixed[i], twice(v_ref[js[i]]))
        trans_ref[js[i]] = rows[i][10:11, C - 1 : C] * eye - times(mixed[i], twice(hk_ref[js[i]]))


def block_totals(trans_ref, write_ref, lev_ref, seg_ref):
    blocks = [(trans_ref[j], write_ref[j]) for j in range(SEG)]
    kept = 0
    while len(blocks) > 1:
        joined = []
        for a in range(0, len(blocks), 2):
            upper = left_form(blocks[a + 1][0])
            lower = [left_form(x) for x in blocks[a]]
            for part in (0, 1):
                lev_ref[kept, part] = lower[part]
            kept += 1
            joined.append((times(upper, twice(lower[0])), times(upper, twice(lower[1])) + blocks[a + 1][1]))
        blocks = joined
    seg_ref[0] = blocks[0][0]
    seg_ref[1] = blocks[0][1]


def level_reads(rows_ref, lev_ref, local_ref, reach_ref):
    kept = 0
    for level in range(1, 5):
        size = 1 << (level - 1)
        for first in range(size, SEG, 2 * size):
            at = pl.ds(first * C, size * C)
            reach = reach_ref[at, :]
            got = times(reach, twice(lev_ref[kept, 1]))
            for d in range(size):
                weight = rows_ref[first + d].T[:, 2 + level : 3 + level]
                local_ref[first + d] = local_ref[first + d] + got[d * C : (d + 1) * C] * weight
            reach_ref[at, :] = left_form(times(reach, twice(lev_ref[kept, 0])))
            kept += 1


def slab_reads(js, taps_ref, rows_ref, x_ref, msg_ref, kt_ref, inv_ref, v_ref, hk_ref, decay_ref, local_ref, reach_ref):
    n = len(js)
    q, cols = [], []
    for j in js:
        c = rows_ref[j].T
        cols.append(c)
        q.append(unit(conv(j, 0, c, taps_ref, x_ref, msg_ref)) * C ** (-0.5))
    attn = [left_form(times(left_form(q[i]), twice(kt_ref[js[i]])) * decay_ref[js[i]]) for i in range(n)]
    attn = [left_form(times(attn[i], twice(inv_ref[js[i]]))) for i in range(n)]
    for i in range(n):
        local_ref[js[i]] = times(attn[i], twice(v_ref[js[i]])) * cols[i][:, 2:3]
        qeff = q[i] * cols[i][:, 10:11] - times(attn[i], twice(hk_ref[js[i]]))
        reach_ref[pl.ds(pl.multiple_of(js[i] * C, C), C), :] = left_form(qeff)


def final(j, s5, s6, gain, rows_ref, local_ref, reach_ref):
    c = rows_ref[j].T
    reach = reach_ref[pl.ds(pl.multiple_of(j * C, C), C), :]
    o = local_ref[j] + times(reach, s5) * c[:, 7:8] + times(reach, s6) * c[:, 8:9]
    return (o * lax.rsqrt(jnp.mean(o * o, axis=1, keepdims=True) + 1e-06) * gain).astype(BF16)


def kernel(
    doc_src, cw_src, gain_src, gates_src, betas_src, weights_src, q_src, k_src, v_src, out_ref,
    doc_ref, taps_ref, gain_ref, raw_ref, tail_ref, pack_ref, msg_ref, x_ref, rows_ref,
    kt_ref, inv_ref, v_ref, hk_ref, decay_ref, trans_ref, write_ref, lev_ref, local_ref, reach_ref,
    seg_ref, far_ref, joint_ref, states_ref, stage_ref,
    load_sem, msg_send, msg_recv, edge_send, in_send, in_recv, far_send, far_recv, out_send, out_recv,
):
    me = lax.axis_index("ctx")
    segment = lax.div(me, SEG)
    mine = lax.rem(me, SEG)
    my_z, my_x, my_core = lax.div(mine, 8), lax.rem(lax.div(mine, 2), 4), lax.rem(mine, 2)
    sources = (q_src, k_src, v_src)

    loads = [
        pltpu.make_async_copy(gates_src, raw_ref.at[0], load_sem.at[0]),
        pltpu.make_async_copy(betas_src, raw_ref.at[1], load_sem.at[1]),
        pltpu.make_async_copy(weights_src, raw_ref.at[pl.ds(2, 7)], load_sem.at[2]),
    ]
    loads += [
        pltpu.make_async_copy(sources[a].at[pl.ds(C - 16, 16), :], tail_ref.at[a], load_sem.at[3 + a]) for a in range(3)
    ]
    small = [
        pltpu.make_async_copy(cw_src.at[:, lanes_ds(SEG * a + mine)], taps_ref.at[a], load_sem.at[6 + a]) for a in range(3)
    ]
    small += [
        pltpu.make_async_copy(gain_src.at[:, lanes_ds(mine)], gain_ref, load_sem.at[9]),
        pltpu.make_async_copy(doc_src, doc_ref, load_sem.at[10]),
    ]
    for copy in loads + small:
        copy.start()

    def place(dz, dx, dc):
        return lax.rem(my_z + dz, 2) * 8 + lax.rem(my_x + dx, 4) * 2 + lax.rem(my_core + dc, 2)

    def at(seg, head):
        return {"ctx": lax.rem(seg, 4) * SEG + head}

    barrier = pltpu.get_barrier_semaphore()

    def greet(target):
        pl.semaphore_signal(barrier, inc=1, device_id=target, device_id_type=pl.DeviceIdType.MESH)

    for n in range(1, 4):
        greet(at(segment + n, mine))
    greet(at(segment + 3, SEG - 1))
    for n in range(1, SEG):
        greet(at(segment, lax.rem(mine + n, SEG)))

    @pl.when(mine == SEG - 1)
    def _():
        for n in range(SEG):
            greet(at(segment + 1, n))

    def keeping(a):
        return pltpu.make_async_copy(sources[a].at[:, lanes_ds(mine)], x_ref.at[mine, a], in_recv.at[mine, a])

    for a in (1, 2, 0):
        keeping(a).start()
    for copy in loads:
        copy.wait()
    for r in range(9):
        pack_ref[:, r, :] = raw_ref[r]
    for h in range(SEG):
        for a in range(3):
            pack_ref[h, 9 + 3 * a : 12 + 3 * a, :] = tail_ref[a, 8:16, h * C : (h + 1) * C].astype(F32)[5:8]
    for r in range(18, 24):
        pack_ref[:, r, :] = jnp.zeros((SEG, C), F32)

    @pl.when(mine == SEG - 1)
    def _():
        pl.semaphore_wait(barrier, 19 + SEG)

    @pl.when(mine != SEG - 1)
    def _():
        pl.semaphore_wait(barrier, 19)

    order = [(dz, dx, dc) for dx in (0, 1, 3, 2) for dz in (0, 1) for dc in (0, 1)][1:]

    def message(head):
        return pltpu.make_async_remote_copy(
            src_ref=pack_ref.at[head], dst_ref=msg_ref.at[mine + 1],
            send_sem=msg_send.at[head], recv_sem=msg_recv.at[mine + 1],
            device_id=at(segment, head), device_id_type=pl.DeviceIdType.MESH,
        )

    def message_from(slab):
        return pltpu.make_async_remote_copy(
            src_ref=pack_ref.at[slab], dst_ref=msg_ref.at[slab + 1],
            send_sem=msg_send.at[slab], recv_sem=msg_recv.at[slab + 1],
            device_id=at(segment, slab), device_id_type=pl.DeviceIdType.MESH,
        )

    own_message = pltpu.make_async_copy(pack_ref.at[mine], msg_ref.at[mine + 1], msg_recv.at[mine + 1])

    def edge(head):
        return pltpu.make_async_remote_copy(
            src_ref=pack_ref.at[head], dst_ref=msg_ref.at[0],
            send_sem=edge_send.at[head], recv_sem=msg_recv.at[0],
            device_id=at(segment + 1, head), device_id_type=pl.DeviceIdType.MESH,
        )

    def sending(a, head):
        return pltpu.make_async_remote_copy(
            src_ref=sources[a].at[:, lanes_ds(head)], dst_ref=x_ref.at[mine, a],
            send_sem=in_send.at[head, a], recv_sem=in_recv.at[mine, a],
            device_id=at(segment, head), device_id_type=pl.DeviceIdType.MESH,
        )

    def arriving(a, slab):
        return pltpu.make_async_remote_copy(
            src_ref=sources[a].at[:, lanes_ds(slab)], dst_ref=x_ref.at[slab, a],
            send_sem=in_send.at[slab, a], recv_sem=in_recv.at[slab, a],
            device_id=at(segment, slab), device_id_type=pl.DeviceIdType.MESH,
        )

    own_message.start()
    for step in order:
        message(place(*step)).start()

    @pl.when(mine == SEG - 1)
    def _():
        for n in range(SEG):
            edge(jnp.int32(n)).start()

    for step in order:
        for a in (1, 2):
            sending(a, place(*step)).start()
    for step in order:
        sending(0, place(*step)).start()

    for copy in small:
        copy.wait()
    own_message.wait()
    for step in order:
        message_from(place(*step)).wait_recv()
    edge(mine).wait_recv()
    fill_rows(segment * (SEG * C), doc_ref, msg_ref, rows_ref)

    def members(m):
        dx = m + lax.div(m, 2) - 2 * lax.div(m, 3)
        x = lax.rem(my_x + 4 - dx, 4)
        return [z * 8 + x * 2 + core for z in (0, 1) for core in (0, 1)]

    def await_inputs(js, arrays):
        for j in js:
            @pl.when(j == mine)
            def _():
                for a in arrays:
                    keeping(a).wait()

            @pl.when(j != mine)
            def _():
                for a in arrays:
                    arriving(a, j).wait_recv()

    def state_group(js):
        await_inputs(js, (1, 2))
        slab_states(
            js, taps_ref, rows_ref, x_ref, msg_ref, kt_ref, inv_ref, v_ref, hk_ref, decay_ref, trans_ref, write_ref
        )

    def early(m, _):
        state_group(members(m))
        return 0

    lax.fori_loop(0, 2, early, 0)
    state_group(members(jnp.int32(2)) + members(jnp.int32(3)))

    def across(n, src, to, slot):
        return pltpu.make_async_remote_copy(
            src_ref=src, dst_ref=far_ref.at[slot], send_sem=far_send.at[n], recv_sem=far_recv.at[slot],
            device_id=at(jnp.int32(to), mine), device_id_type=pl.DeviceIdType.MESH,
        )

    block_totals(trans_ref, write_ref, lev_ref, seg_ref)
    first_write = across(0, seg_ref.at[1], 1, 0)
    third_trans = across(1, seg_ref.at[0], 3, 1)
    third_write = across(2, seg_ref.at[1], 3, 2)
    to_third = across(3, joint_ref, 2, 3)
    to_fourth = across(4, joint_ref, 3, 3)

    @pl.when(segment == 0)
    def _():
        first_write.start()

    @pl.when(segment == 2)
    def _():
        third_trans.start()
        third_write.start()

    states_ref[...] = jnp.zeros_like(states_ref)

    def read_group(m, _):
        @pl.when((segment == 1) & (m == 1))
        def _():
            first_write.wait_recv()
            states_ref[0] = far_ref[0]
            joint_ref[...] = times(left_form(seg_ref[0]), right_form(far_ref[0])) + seg_ref[1]
            to_fourth.start()
            to_third.start()

        js = members(2 * m) + members(2 * m + 1)
        await_inputs(js, (0,))
        slab_reads(
            js, taps_ref, rows_ref, x_ref, msg_ref,
            kt_ref, inv_ref, v_ref, hk_ref, decay_ref, local_ref, reach_ref,
        )
        return 0

    lax.fori_loop(0, 2, read_group, 0)
    level_reads(rows_ref, lev_ref, local_ref, reach_ref)

    @pl.when(segment == 2)
    def _():
        to_third.wait_recv()
        states_ref[1] = far_ref[3]

    @pl.when(segment == 3)
    def _():
        third_trans.wait_recv()
        third_write.wait_recv()
        states_ref[0] = far_ref[2]
        to_fourth.wait_recv()
        states_ref[1] = times(left_form(far_ref[1]), right_form(far_ref[3]))

    gain = gain_ref[...]
    s5 = right_form(states_ref[0])
    s6 = right_form(states_ref[1])

    def leaving(slab):
        return pltpu.make_async_remote_copy(
            src_ref=stage_ref.at[slab], dst_ref=out_ref.at[:, lanes_ds(mine)],
            send_sem=out_send.at[slab], recv_sem=out_recv.at[mine],
            device_id=at(segment, slab), device_id_type=pl.DeviceIdType.MESH,
        )

    def returning(head):
        return pltpu.make_async_remote_copy(
            src_ref=stage_ref.at[head], dst_ref=out_ref.at[:, lanes_ds(head)],
            send_sem=out_send.at[head], recv_sem=out_recv.at[head],
            device_id=at(segment, head), device_id_type=pl.DeviceIdType.MESH,
        )

    for dx in (2, 1, 3, 0):
        js = [place(dz, dx, dc) for dz in (1, 0) for dc in (1, 0)]
        for j in js:
            stage_ref[j] = final(j, s5, s6, gain, rows_ref, local_ref, reach_ref)
        for j in js[: 4 if dx else 3]:
            leaving(j).start()
    home = pltpu.make_async_copy(stage_ref.at[mine], out_ref.at[:, lanes_ds(mine)], out_recv.at[mine])
    home.start()
    home.wait()
    for step in order:
        returning(place(*step)).wait_recv()

    for step in order:
        head = place(*step)
        message(head).wait_send()
        for a in range(3):
            sending(a, head).wait_send()
        leaving(head).wait_send()

    @pl.when(mine == SEG - 1)
    def _():
        for n in range(SEG):
            edge(jnp.int32(n)).wait_send()

    @pl.when(segment == 0)
    def _():
        first_write.wait_send()

    @pl.when(segment == 1)
    def _():
        to_third.wait_send()
        to_fourth.wait_send()

    @pl.when(segment == 2)
    def _():
        third_trans.wait_send()
        third_write.wait_send()


def body(queries, keys, values_in, conv_weights, log_gates, betas, level_weights, doc_lengths, out_gain):
    square = pltpu.VMEM((SEG, C, C), F32)
    wide = pltpu.VMEM((SEG, C, 2 * C), BF16)
    hbm = pl.BlockSpec(memory_space=pl.ANY)
    dma = pltpu.SemaphoreType.DMA
    return pl.pallas_call(
        kernel,
        out_shape=jax.ShapeDtypeStruct(queries.shape, BF16),
        in_specs=[hbm] * 9,
        out_specs=hbm,
        scratch_shapes=[
            pltpu.SMEM(doc_lengths.shape, jnp.int32),
            pltpu.VMEM((3, 4, C), F32),
            pltpu.VMEM((1, C), F32),
            pltpu.VMEM((9, SEG, C), F32),
            pltpu.VMEM((3, 16, queries.shape[1]), BF16),
            pltpu.VMEM((SEG, 24, C), F32),
            pltpu.VMEM((SEG + 1, 24, C), F32),
            pltpu.VMEM((SEG, 3, C, C), BF16),
            pltpu.VMEM((SEG, 16, C), F32),
            wide, wide, wide, wide, square, square, square,
            pltpu.VMEM((SEG - 1, 2, C, 2 * C), BF16),
            square,
            pltpu.VMEM((SEG * C, 2 * C), BF16),
            pltpu.VMEM((2, C, C), F32),
            pltpu.VMEM((4, C, C), F32),
            pltpu.VMEM((C, C), F32),
            pltpu.VMEM((2, C, C), F32),
            pltpu.VMEM((SEG, C, C), BF16),
            dma((11,)), dma((SEG,)), dma((SEG + 1,)), dma((SEG,)), dma((SEG, 3)), dma((SEG, 3)),
            dma((5,)), dma((4,)), dma((SEG,)), dma((SEG,)),
        ],
        compiler_params=pltpu.CompilerParams(
            collective_id=0, has_side_effects=True, vmem_limit_bytes=60 << 20
        ),
    )(
        doc_lengths, conv_weights, out_gain[None, :], log_gates, betas, level_weights, queries, keys, values_in
    )


def solution(mesh):
    in_specs = (
        P(("dp", "ctx"), None),
        P(("dp", "ctx"), None),
        P(("dp", "ctx"), None),
        P(),
        P(None, ("dp", "ctx")),
        P(None, ("dp", "ctx")),
        P(None, None, ("dp", "ctx")),
        P("dp"),
        P(),
    )
    out_specs = P(("dp", "ctx"), None)
    return jax.shard_map(body, mesh=mesh, in_specs=in_specs, out_specs=out_specs, check_vma=False)
```
